32 devices in a mesh: phase: 2 (over x), dp: 4 (over y, core), mp: 4 (over z).
Axes of the slice: x: 2, y: 2, z: 4, core: 2. Of those that a mesh axis runs over, the one named last changes fastest.
Arguments:
- memory: bfloat16 [4, 256, 1024], P('dp', None, 'mp'), may hold values from -6 to 6
- states: bfloat16 [2, 4, 256, 1024], P('phase', 'dp', None, 'mp'), may hold values from -6 to 6
- targets: bfloat16 [2, 4, 256, 1024], P('phase', 'dp', None, 'mp'), may hold values from -6 to 6
- w_query: bfloat16 [2, 1024, 16384], P('phase', None, 'mp'), may hold values from -0.1875 to 0.1875
- w_key: bfloat16 [2, 1024, 16384], P('phase', None, 'mp'), may hold values from -0.1875 to 0.1875
- w_value: bfloat16 [2, 1024, 16384], P('phase', None, 'mp'), may hold values from -0.1875 to 0.1875
- w_out: bfloat16 [2, 16384, 1024], P('phase', 'mp'), may hold values from -0.046875 to 0.046875
- src_ids: int32 [4, 256], P('dp'), may hold values from 0 to 3, never falling along the last dimension, each value on 1 to 128 neighbouring positions
- tgt_ids: int32 [4, 256], P('dp'), may hold values from 0 to 3, never falling along the last dimension, each value on 1 to 128 neighbouring positions
- counts: int32 [4], P('dp'), may hold values from 1 to 256
Outputs:
- cross_out: bfloat16 [2, 4, 256, 1024], P('phase', 'dp', None, 'mp')
- loss: float32 [2], P('phase')
- states_grad: bfloat16 [2, 4, 256, 1024], P('phase', 'dp', None, 'mp')
- memory_grad: bfloat16 [4, 256, 1024], P('dp', None, 'mp')
The draws below stay inside these ranges and needn't reach their ends.
Inputs may be any that keep to these rules, and one draw needn't show every extreme that they name: `src_ids`: both id arrays of a sample hold all segment numbers 0 to 3.
All inputs are finite; a program needn't handle non-finite values.
Results may differ from the reference program's by a relative error of at most 0.013.
The reference program's roundings to bfloat16 on the way count: a program that leaves them out, or rounds other values in their place, can miss the bound.
Values may be sent and summed in bfloat16 or wider, within the bound.
No kernel may reach another device: no remote copies, remote signals or barrier semaphores. Data moves between devices by JAX's collectives and lax.ppermute only.
A program may use at most 128 MiB of HBM per device.

```python
import math
import jax
import jax.numpy as jnp
import numpy as np
from jax import lax

D = 1024
HEADS = 128
HEAD = 128
SRC = 256
TGT = 256
INNER = 16384
BATCH = 4
N_PHASE = 2


def draw_states(key, part):
    base = jax.random.normal(jax.random.fold_in(key, 11), (N_PHASE, BATCH, TGT, D), jnp.float32)
    return jnp.clip(base, -6.0, 6.0).astype(jnp.bfloat16)


def place_ends(array, own_key, least, largest):
    shape = array.shape
    spot = [jax.random.randint(jax.random.fold_in(own_key, axis), (), 0, shape[axis]) for axis in range(len(shape))]
    array = array.at[tuple(spot)].set(least)
    longest = shape.index(max(shape))
    spot[longest] = (spot[longest] + 1) % shape[longest]
    return array.at[tuple(spot)].set(largest)


def level_of(stream_key, shape, cuts, low, high):
    gain, own = 1.0, jax.random.fold_in(stream_key, 6)
    for axis_at, parts in cuts:
        steps = jnp.exp(jax.random.uniform(jax.random.fold_in(own, axis_at), (parts,), jnp.float32, low / len(cuts), high / len(cuts)))
        gain = gain * jnp.repeat(steps, shape[axis_at] // parts).reshape([-1 if axis == axis_at else 1 for axis in range(len(shape))])
    return gain


def split_up(count, total, reach, slope):
    loads = [(1 << 20) // math.isqrt(grade ** slope) + 1 for grade in range(2, count + 1)]
    surplus, holding = total - reach - (count - 1), [1] * (count - 1)
    while surplus > 0:
        free = [i for i in range(count - 1) if holding[i] < reach]
        whole, budget = sum([loads[i] for i in free]), surplus
        for i in free:
            extra = min(reach - holding[i], max(1, budget * loads[i] // whole), surplus)
            holding[i] = holding[i] + extra
            surplus = surplus - extra
    return np.array([reach] + holding)


def uneven_parts(key, count, total, most, slope):
    if count == 2:
        one = jax.random.randint(key, (), max(1, total - most), min(most, total - 1) + 1)
        return jnp.stack([one, total - one])
    lengths = jnp.asarray(split_up(count, total, most, slope), jnp.int32)
    pairs = (count - 1) // 2
    source_of, receiver = lengths[1:1 + 2 * pairs:2], lengths[2:2 + 2 * pairs:2]
    slack = jnp.minimum(source_of - 1, most - receiver)
    passed = jax.random.randint(jax.random.fold_in(key, 1), (pairs,), 0, 1 << 20) % (slack + 1)
    lengths = lengths.at[1:1 + 2 * pairs:2].set(source_of - passed).at[2:2 + 2 * pairs:2].set(receiver + passed)
    return lengths[jax.random.permutation(jax.random.fold_in(key, 2), count)]


def centred(rng, shape, scale, limit, split=(), dtype=jnp.bfloat16):
    result = jax.random.normal(rng, shape, jnp.float32) * scale
    if len(split) > 0:
        result = level_of(rng, shape, split, -0.22, 0.18) * result
    return jnp.clip(result, min=-limit, max=limit).astype(dtype)


def setup_inputs(seed: int = 0) -> dict:
    keys = jax.random.split(jax.random.key(seed), 11)
    memory = centred(keys[0], (BATCH, SRC, D), 1.0, 6.0, ((0, 4), (2, 4)))
    states = draw_states(jax.random.fold_in(keys[10], 71), 0)
    targets = centred(keys[2], (N_PHASE, BATCH, TGT, D), 1.0, 6.0, ((0, 2), (1, 4), (3, 4)))
    w_query = centred(keys[3], (N_PHASE, D, INNER), D ** -0.5, 0.1875, ((0, 2), (2, 4)))
    w_key = centred(keys[4], (N_PHASE, D, INNER), D ** -0.5, 0.1875, ((0, 2), (2, 4)))
    w_value = centred(keys[5], (N_PHASE, D, INNER), D ** -0.5, 0.1875, ((0, 2), (2, 4)))
    w_out = centred(keys[6], (N_PHASE, INNER, D), INNER ** -0.5, 0.046875, ((0, 2), (1, 4)))
    src_ids = jax.vmap(lambda own: jnp.searchsorted(jnp.cumsum(uneven_parts(own, 4, SRC, SRC // 2, 1)), jnp.arange(SRC), side="right"))(jax.random.split(keys[7], BATCH)).reshape((BATCH, SRC)).astype(jnp.int32)
    tgt_ids = jax.vmap(lambda own: jnp.searchsorted(jnp.cumsum(uneven_parts(own, 4, TGT, TGT // 2, 1)), jnp.arange(TGT), side="right"))(jax.random.split(keys[8], BATCH)).reshape((BATCH, TGT)).astype(jnp.int32)
    counts = place_ends(jax.random.randint(keys[9], (BATCH,), 1, TGT + 1), jax.random.fold_in(keys[9], 1), 1, TGT).astype(jnp.int32)
    return dict(memory=memory, states=states, targets=targets, w_query=w_query, w_key=w_key, w_value=w_value, w_out=w_out, src_ids=src_ids, tgt_ids=tgt_ids, counts=counts)


def sample_pass(x, mem, tgt, src_id, tgt_id, count, wq, wk, wv, wo):
    q = jnp.dot(x, wq, preferred_element_type=jnp.float32).astype(jnp.bfloat16).reshape(TGT, HEADS, HEAD)
    k = jnp.dot(mem, wk, preferred_element_type=jnp.float32).astype(jnp.bfloat16).reshape(SRC, HEADS, HEAD)
    v = jnp.dot(mem, wv, preferred_element_type=jnp.float32).astype(jnp.bfloat16).reshape(SRC, HEADS, HEAD)
    qf = q.astype(jnp.float32)
    kf = k.astype(jnp.float32)
    vf = v.astype(jnp.float32)
    scores = jnp.einsum('the,jhe->htj', qf, kf)
    allowed = tgt_id[:, None] == src_id[None, :]
    scores = jnp.where(allowed[None], scores, -1e30)
    probs = jax.nn.softmax(scores, axis=-1)
    pb = probs.astype(jnp.bfloat16)
    pbf = pb.astype(jnp.float32)
    attended = jnp.einsum('htj,jhe->the', pbf, vf).astype(jnp.bfloat16).reshape(TGT, HEADS * HEAD)
    out = jnp.dot(attended, wo, preferred_element_type=jnp.float32).astype(jnp.bfloat16)
    valid = (jnp.arange(TGT) < count).astype(jnp.bfloat16)
    grad_out = tgt * valid[:, None]
    part = jnp.sum(out.astype(jnp.float32) * grad_out.astype(jnp.float32))
    grad_att = jnp.dot(grad_out, wo.T, preferred_element_type=jnp.float32).astype(jnp.bfloat16).reshape(TGT, HEADS, HEAD)
    gaf = grad_att.astype(jnp.float32)
    grad_prob = jnp.einsum('the,jhe->htj', gaf, vf)
    inner = jnp.sum(probs * grad_prob, axis=-1, keepdims=True)
    grad_score = (probs * (grad_prob - inner)).astype(jnp.bfloat16).astype(jnp.float32)
    grad_q = jnp.einsum('htj,jhe->the', grad_score, kf).astype(jnp.bfloat16).reshape(TGT, HEADS * HEAD)
    grad_k = jnp.einsum('htj,the->jhe', grad_score, qf).astype(jnp.bfloat16).reshape(SRC, HEADS * HEAD)
    grad_v = jnp.einsum('htj,the->jhe', pbf, gaf).astype(jnp.bfloat16).reshape(SRC, HEADS * HEAD)
    grad_x = jnp.dot(grad_q, wq.T, preferred_element_type=jnp.float32)
    grad_m = jnp.dot(grad_k, wk.T, preferred_element_type=jnp.float32) + jnp.dot(grad_v, wv.T, preferred_element_type=jnp.float32)
    return out, part, grad_x, grad_m


def reference(memory, states, targets, w_query, w_key, w_value, w_out, src_ids, tgt_ids, counts):
    total = jnp.sum(counts.astype(jnp.float32))
    outs = []
    losses = []
    state_grads = []
    mem_grad = jnp.zeros((BATCH, SRC, D), jnp.float32)
    for section in range(N_PHASE):
        def one(items):
            x, mem, tgt, sid, tid, cnt = items
            return sample_pass(x, mem, tgt, sid, tid, cnt, w_query[section], w_key[section], w_value[section], w_out[section])
        out, part, grad_x, grad_m = lax.map(one, (states[section], memory, targets[section], src_ids, tgt_ids, counts))
        outs.append(out)
        losses.append(jnp.sum(part) / total)
        state_grads.append((grad_x / total).astype(jnp.bfloat16))
        mem_grad = mem_grad + grad_m
    return jnp.stack(outs), jnp.stack(losses), jnp.stack(state_grads), (mem_grad / total).astype(jnp.bfloat16)
```

```python
import functools

import jax
import jax.numpy as jnp
from jax import lax
from jax.experimental import pallas as pl
from jax.experimental.pallas import tpu as pltpu
from jax.sharding import PartitionSpec as P

HEAD = 128
EXCLUDED = -1e30
F32 = jnp.float32
BF16 = jnp.bfloat16
VMEM_LIMIT = 60 * 1024 * 1024


def block_width(inner):
    for width in (512, 256):
        if inner % width == 0:
            return width
    return HEAD


def nt(a, b):
    return lax.dot_general(a, b, (((1,), (1,)), ((), ())), preferred_element_type=F32)


def nn(a, b):
    return lax.dot_general(a, b, (((1,), (0,)), ((), ())), preferred_element_type=F32)


def tn(a, b):
    return lax.dot_general(a, b, (((0,), (0,)), ((), ())), preferred_element_type=F32)


def row_copies(idx, hbm, buf, sem, pieces, chunk, width, g):
    return [
        pltpu.make_async_copy(
            hbm.at[pl.ds(pl.multiple_of(idx[s] * chunk, chunk), chunk), pl.ds(pl.multiple_of(g * width, width), width)],
            buf.at[g, pl.ds(s * chunk, chunk), :],
            sem.at[g, s],
        )
        for s in range(pieces)
    ]


def column_copies(idx, hbm, buf, sem, pieces, chunk, width, g):
    return [
        pltpu.make_async_copy(
            hbm.at[pl.ds(pl.multiple_of(g * width, width), width), pl.ds(pl.multiple_of(idx[s] * chunk, chunk), chunk)],
            buf.at[g, :, pl.ds(s * chunk, chunk)],
            sem.at[g, s],
        )
        for s in range(pieces)
    ]


def start_all(blocks, makers):
    @pl.loop(0, blocks)
    def _(g):
        for make in makers:
            for copy in make(g):
                copy.start()


def wait_all(copies):
    for copy in copies:
        copy.wait()


def kv_kernel(pieces, idx, *refs):
    parts, (wk, wv, k_out, v_out, cat, kbuf, vbuf, ksem, vsem) = refs[:pieces], refs[pieces:]
    g, blocks = pl.program_id(0), pl.num_programs(0)
    chunk, width = parts[0].shape[1], k_out.shape[1]
    make_k = functools.partial(row_copies, idx, wk, kbuf, ksem, pieces, chunk, width)
    make_v = functools.partial(row_copies, idx, wv, vbuf, vsem, pieces, chunk, width)

    @pl.when(g == 0)
    def _():
        start_all(blocks, (make_k, make_v))
        for s in range(pieces):
            cat[:, s * chunk : (s + 1) * chunk] = parts[s][...]

    wait_all(make_k(g))
    k_out[...] = nn(cat[...], kbuf[g]).astype(BF16)
    wait_all(make_v(g))
    v_out[...] = nn(cat[...], vbuf[g]).astype(BF16)


def forward_kernel(pieces, idx, *refs):
    parts = refs[:pieces]
    src, tgt, k, v, wq, wo, q_out, p_out = refs[pieces : pieces + 8]
    outs = refs[pieces + 8 : 2 * pieces + 8]
    cat, bias, acc, qbuf, obuf, qsem, osem = refs[2 * pieces + 8 :]
    g, blocks = pl.program_id(0), pl.num_programs(0)
    chunk, width = parts[0].shape[1], q_out.shape[1]
    make_q = functools.partial(row_copies, idx, wq, qbuf, qsem, pieces, chunk, width)
    make_o = functools.partial(column_copies, idx, wo, obuf, osem, pieces, chunk, width)

    @pl.when(g == 0)
    def _():
        start_all(blocks, (make_q, make_o))
        for s in range(pieces):
            cat[:, s * chunk : (s + 1) * chunk] = parts[s][...]
        bias[...] = jnp.where(src[...] == tgt[...], 0.0, EXCLUDED).astype(F32)
        acc[...] = jnp.zeros_like(acc)

    wait_all(make_q(g))
    q = nn(cat[...], qbuf[g]).astype(BF16)
    q_out[...] = q
    attended = []
    for h in range(width // HEAD):
        at = slice(h * HEAD, (h + 1) * HEAD)
        scores = nt(k[:, at], q[:, at]) + bias[...]
        weights = jnp.exp(scores - jnp.max(scores, axis=0, keepdims=True))
        probs = weights * (1.0 / jnp.sum(weights, axis=0, keepdims=True))
        p_out[h] = probs
        attended.append(tn(probs.astype(BF16), v[:, at]).astype(BF16))
    wait_all(make_o(g))
    acc[...] += nn(jnp.concatenate(attended, axis=1), obuf[g])

    @pl.when(g == blocks - 1)
    def _():
        for s in range(pieces):
            outs[s][...] = acc[:, s * chunk : (s + 1) * chunk].astype(outs[s].dtype)


def backward_kernel(pieces, idx, count, *refs):
    parts = refs[:pieces]
    q, k, v, p, wq, wo, dk_out, dv_out = refs[pieces : pieces + 8]
    outs = refs[pieces + 8 : 2 * pieces + 8]
    cat, acc, qbuf, obuf, qsem, osem = refs[2 * pieces + 8 :]
    g, blocks = pl.program_id(0), pl.num_programs(0)
    chunk, width = parts[0].shape[1], q.shape[1]
    make_q = functools.partial(row_copies, idx, wq, qbuf, qsem, pieces, chunk, width)
    make_o = functools.partial(column_copies, idx, wo, obuf, osem, pieces, chunk, width)

    @pl.when(g == 0)
    def _():
        start_all(blocks, (make_o, make_q))
        valid = lax.broadcasted_iota(jnp.int32, parts[0].shape, 0) < count[0]
        for s in range(pieces):
            cat[:, s * chunk : (s + 1) * chunk] = jnp.where(valid, parts[s][...], jnp.zeros_like(parts[s]))
        acc[...] = jnp.zeros_like(acc)

    wait_all(make_o(g))
    grad_att = nt(cat[...], obuf[g]).astype(BF16)
    grad_q = []
    for h in range(width // HEAD):
        at = slice(h * HEAD, (h + 1) * HEAD)
        probs = p[h]
        grad_prob = nt(v[:, at], grad_att[:, at])
        inner = jnp.sum(probs * grad_prob, axis=0, keepdims=True)
        grad_score = (probs * (grad_prob - inner)).astype(BF16)
        grad_q.append(tn(grad_score, k[:, at]).astype(BF16))
        dk_out[:, at] = nn(grad_score, q[:, at]).astype(BF16)
        dv_out[:, at] = nn(probs.astype(BF16), grad_att[:, at]).astype(BF16)
    wait_all(make_q(g))
    acc[...] += nt(jnp.concatenate(grad_q, axis=1), qbuf[g])

    @pl.when(g == blocks - 1)
    def _():
        for s in range(pieces):
            outs[s][...] = acc[:, s * chunk : (s + 1) * chunk].astype(outs[s].dtype)


def memory_kernel(which, chunk, idx, dk, dv, wk, wv, *refs):
    outs, (kbuf, vbuf, ksem, vsem) = refs[: len(which)], refs[len(which) :]

    def copies(i):
        rows = pl.ds(pl.multiple_of(idx[which[i]] * chunk, chunk), chunk)
        return (
            pltpu.make_async_copy(wk.at[rows, :], kbuf.at[i], ksem.at[i]),
            pltpu.make_async_copy(wv.at[rows, :], vbuf.at[i], vsem.at[i]),
        )

    for i in range(len(which)):
        for copy in copies(i):
            copy.start()
    for i in range(len(which)):
        wait_all(copies(i))
        outs[i][...] = (nt(dk[...], kbuf[i]) + nt(dv[...], vbuf[i])).astype(outs[i].dtype)


def whole(shape):
    return pl.BlockSpec(shape, lambda *_: (0,) * len(shape))


ANY = pl.BlockSpec(memory_space=pl.ANY)
SMEM = pl.BlockSpec(memory_space=pltpu.SMEM)


def params():
    return pltpu.CompilerParams(vmem_limit_bytes=VMEM_LIMIT)


def cost(flops, bytes_accessed, transcendentals=0):
    return pl.CostEstimate(flops=flops, bytes_accessed=bytes_accessed, transcendentals=transcendentals)


def piece_types(rows, chunk, pieces, first=0):
    return [jax.ShapeDtypeStruct((rows, chunk), F32 if s == 0 else BF16) for s in range(first, pieces)]


def project_kv(idx, parts, wk, wv):
    pieces, (rows, chunk), (features, inner) = len(parts), parts[0].shape, wk.shape
    width = block_width(inner)
    blocks = inner // width
    column = pl.BlockSpec((rows, width), lambda g: (0, g))
    return pl.pallas_call(
        functools.partial(kv_kernel, pieces),
        grid=(blocks,),
        in_specs=[SMEM] + [whole((rows, chunk))] * pieces + [ANY, ANY],
        out_specs=[column, column],
        out_shape=[jax.ShapeDtypeStruct((rows, inner), BF16)] * 2,
        scratch_shapes=[
            pltpu.VMEM((rows, features), BF16),
            pltpu.VMEM((blocks, features, width), BF16),
            pltpu.VMEM((blocks, features, width), BF16),
            pltpu.SemaphoreType.DMA((blocks, pieces)),
            pltpu.SemaphoreType.DMA((blocks, pieces)),
        ],
        compiler_params=params(),
        cost_estimate=cost(4 * rows * features * inner, 4 * features * inner),
        name="project_kv",
    )(idx, *parts, wk, wv)


def attend(idx, parts, src, tgt, k, v, wq, wo):
    pieces, (rows, chunk), (features, inner) = len(parts), parts[0].shape, wq.shape
    src_len = k.shape[0]
    width = block_width(inner)
    blocks, heads = inner // width, width // HEAD
    key_block = pl.BlockSpec((src_len, width), lambda g: (0, g))
    query_block = pl.BlockSpec((rows, width), lambda g: (0, g))
    prob_block = pl.BlockSpec((heads, src_len, rows), lambda g: (g, 0, 0))
    return pl.pallas_call(
        functools.partial(forward_kernel, pieces),
        grid=(blocks,),
        in_specs=[SMEM]
        + [whole((rows, chunk))] * pieces
        + [whole((src_len, 1)), whole((1, rows)), key_block, key_block, ANY, ANY],
        out_specs=[query_block, prob_block] + [whole((rows, chunk))] * pieces,
        out_shape=[
            jax.ShapeDtypeStruct((rows, inner), BF16),
            jax.ShapeDtypeStruct((inner // HEAD, src_len, rows), F32),
        ]
        + piece_types(rows, chunk, pieces),
        scratch_shapes=[
            pltpu.VMEM((rows, features), BF16),
            pltpu.VMEM((src_len, rows), F32),
            pltpu.VMEM((rows, features), F32),
            pltpu.VMEM((blocks, features, width), BF16),
            pltpu.VMEM((blocks, width, features), BF16),
            pltpu.SemaphoreType.DMA((blocks, pieces)),
            pltpu.SemaphoreType.DMA((blocks, pieces)),
        ],
        compiler_params=params(),
        cost_estimate=cost(6 * rows * features * inner, 8 * features * inner),
        name="attend",
    )(idx, *parts, src, tgt, k, v, wq, wo)


def attend_backward(idx, count, parts, q, k, v, p, wq, wo):
    pieces, (rows, chunk), (features, inner) = len(parts), parts[0].shape, wq.shape
    src_len = k.shape[0]
    width = block_width(inner)
    blocks, heads = inner // width, width // HEAD
    key_block = pl.BlockSpec((src_len, width), lambda g: (0, g))
    query_block = pl.BlockSpec((rows, width), lambda g: (0, g))
    prob_block = pl.BlockSpec((heads, src_len, rows), lambda g: (g, 0, 0))
    return pl.pallas_call(
        functools.partial(backward_kernel, pieces),
        grid=(blocks,),
        in_specs=[SMEM, SMEM]
        + [whole((rows, chunk))] * pieces
        + [query_block, key_block, key_block, prob_block, ANY, ANY],
        out_specs=[key_block, key_block] + [whole((rows, chunk))] * pieces,
        out_shape=[jax.ShapeDtypeStruct((src_len, inner), BF16)] * 2 + piece_types(rows, chunk, pieces),
        scratch_shapes=[
            pltpu.VMEM((rows, features), BF16),
            pltpu.VMEM((rows, features), F32),
            pltpu.VMEM((blocks, features, width), BF16),
            pltpu.VMEM((blocks, width, features), BF16),
            pltpu.SemaphoreType.DMA((blocks, pieces)),
            pltpu.SemaphoreType.DMA((blocks, pieces)),
        ],
        compiler_params=params(),
        cost_estimate=cost(8 * rows * features * inner, 8 * features * inner),
        name="attend_backward",
    )(idx, count, *parts, q, k, v, p, wq, wo)


def memory_grads(idx, which, chunk, dk, dv, wk, wv):
    rows, inner = dk.shape
    full = pl.BlockSpec(memory_space=pltpu.VMEM)
    return pl.pallas_call(
        functools.partial(memory_kernel, which, chunk),
        in_specs=[SMEM, full, full, ANY, ANY],
        out_specs=[full] * len(which),
        out_shape=[jax.ShapeDtypeStruct((rows, chunk), F32 if s == 0 else BF16) for s in which],
        scratch_shapes=[
            pltpu.VMEM((len(which), chunk, inner), BF16),
            pltpu.VMEM((len(which), chunk, inner), BF16),
            pltpu.SemaphoreType.DMA((len(which),)),
            pltpu.SemaphoreType.DMA((len(which),)),
        ],
        compiler_params=params(),
        cost_estimate=cost(4 * rows * chunk * len(which) * inner, 4 * chunk * len(which) * inner),
        name="memory_grads",
    )(idx, dk, dv, wk, wv)


def swap(x, axis, step):
    size = lax.axis_size(axis)
    return lax.ppermute(x, axis, [(i, i ^ step) for i in range(size)])


def butterfly(x, axis):
    step = 1
    while step < lax.axis_size(axis):
        x = x + swap(x, axis, step)
        step *= 2
    return x


def local(direct, memory, states, targets, w_query, w_key, w_value, w_out, src_ids, tgt_ids, counts):
    n = lax.axis_size("mp")
    mem, state, target = memory[0], states[0, 0], targets[0, 0]
    wq, wk, wv, wo = w_query[0], w_key[0], w_value[0], w_out[0]
    chunk = mem.shape[1]
    valid = jnp.arange(target.shape[0])[:, None] < counts[0]
    grad_own = jnp.where(valid, target, jnp.zeros_like(target)).astype(F32)
    src, tgt = src_ids.reshape(-1, 1), tgt_ids.reshape(1, -1)
    if direct:
        idx = lax.axis_index("mp") ^ jnp.arange(n, dtype=jnp.int32)

        def gather(x):
            return [x] + [swap(x, "mp", s) for s in range(1, n)]

        def scatter(parts):
            total = parts[0]
            for s in range(1, n):
                total = total + swap(parts[s], "mp", s).astype(F32)
            return total
    else:
        idx = jnp.zeros((1,), jnp.int32)
        chunk = chunk * n

        def gather(x):
            return [lax.all_gather(x, "mp", axis=1, tiled=True)]

        def scatter(parts):
            return lax.psum_scatter(parts[0], "mp", scatter_dimension=1, tiled=True)

    pieces = n if direct else 1
    mem_parts, state_parts, target_parts = gather(mem), gather(state), gather(target)
    k, v = project_kv(idx, mem_parts, wk, wv)
    q, p, *out_parts = attend(idx, state_parts, src, tgt, k, v, wq, wo)
    out_low = scatter(out_parts).astype(BF16)
    dk, dv, *grad_x_parts = attend_backward(idx, counts, target_parts, q, k, v, p, wq, wo)
    grad_x = scatter(grad_x_parts)
    grad_m_parts = memory_grads(idx, tuple(range(pieces)), chunk, dk, dv, wk, wv)
    grad_m = scatter(grad_m_parts)

    loss_part = jnp.sum(out_low.astype(F32) * grad_own)
    count_part = counts[0].astype(F32) / n
    if direct:
        sums = butterfly(butterfly(jnp.stack([loss_part, count_part]), "mp"), "dp")
        loss_total, count_total = sums[0], sums[1]
        grad_m = lax.reduce_precision(grad_m, 8, 7)
        grad_m = grad_m + swap(grad_m.astype(BF16), "phase", 1).astype(F32)
    else:
        loss_total, count_total = lax.psum((loss_part, count_part), ("dp", "mp"))
        grad_m = lax.psum(grad_m, "phase")
    loss = (loss_total / count_total).reshape(1)
    states_grad = (grad_x / count_total).astype(BF16)
    memory_grad = (grad_m / count_total).astype(BF16)
    return out_low[None, None], loss, states_grad[None, None], memory_grad[None]


def power_of_two(size):
    return size & (size - 1) == 0


def solution(mesh):
    sizes = mesh.shape
    placed = (
        P("dp", None, "mp"),
        P("phase", "dp", None, "mp"),
        P("phase", "dp", None, "mp"),
        P("phase", None, "mp"),
        P("phase", None, "mp"),
        P("phase", None, "mp"),
        P("phase", "mp", None),
        P("dp", None),
        P("dp", None),
        P("dp"),
    )
    direct = 1 < sizes["mp"] <= 4 and power_of_two(sizes["mp"]) and power_of_two(sizes["dp"]) and sizes["phase"] == 2
    return jax.shard_map(
        functools.partial(local, direct),
        mesh=mesh,
        in_specs=placed,
        out_specs=(
            P("phase", "dp", None, "mp"),
            P("phase"),
            P("phase", "dp", None, "mp"),
            P("dp", None, "mp"),
        ),
        check_vma=False,
    )
```

```python
import functools

import jax
import jax.numpy as jnp
from jax import lax
from jax.experimental import pallas as pl
from jax.experimental.pallas import tpu as pltpu
from jax.sharding import PartitionSpec as P


HEAD = 128
EXCLUDED = -1e30
F32 = jnp.float32
BF16 = jnp.bfloat16


def block_width(inner):
    for width in (512, 256):
        if inner % width == 0:
            return width
    return HEAD


def nt(a, b):
    return lax.dot_general(a, b, (((1,), (1,)), ((), ())), preferred_element_type=F32)


def nn(a, b):
    return lax.dot_general(a, b, (((1,), (0,)), ((), ())), preferred_element_type=F32)


def tn(a, b):
    return lax.dot_general(a, b, (((0,), (0,)), ((), ())), preferred_element_type=F32)


def columns_of(idx, s, chunk):
    return pl.ds(pl.multiple_of(idx[s] * chunk, chunk), chunk)


def join(idx, cat, parts, value=lambda x: x):
    chunk = parts[0].shape[1]
    for s in range(len(parts)):
        cat[:, columns_of(idx, s, chunk)] = value(parts[s][...])


def load_kernel(*refs):
    half = (len(refs) - 1) // 2
    sources, targets, sems = refs[:half], refs[half:-1], refs[-1]
    copies = []
    for i in range(half):
        rows = sources[i].shape[0] // LOAD_PARTS
        for j in range(LOAD_PARTS):
            at = pl.ds(j * rows, rows)
            copies.append(pltpu.make_async_copy(sources[i].at[at, :], targets[i].at[at, :], sems.at[i, j]))
    for copy in copies:
        copy.start()
    for copy in copies:
        copy.wait()


def blocks_of(inner, width, body):
    @pl.loop(0, inner // width)
    def _(g):
        body(pl.ds(pl.multiple_of(g * width, width), width), g)


def kv_kernel(pieces, idx, *refs):
    parts, (wk, wv, k, v, cat) = refs[:pieces], refs[pieces:]
    inner = wk.shape[1]
    join(idx, cat, parts)

    def body(at, g):
        k[:, at] = nn(cat[...], wk[:, at]).astype(BF16)
        v[:, at] = nn(cat[...], wv[:, at]).astype(BF16)

    blocks_of(inner, block_width(inner), body)


def softmax_terms(k, q, bias):
    scores = nt(k, q) + bias
    top = jnp.max(scores, axis=0, keepdims=True)
    weights = jnp.exp(scores - top)
    return weights, top, 1.0 / jnp.sum(weights, axis=0, keepdims=True)


def head_loop(inner, body):
    heads = head_group(inner)

    @pl.loop(0, inner // HEAD // heads)
    def _(i):
        for j in range(heads):
            h = i * heads + j
            body(pl.ds(pl.multiple_of(h * HEAD, HEAD), HEAD), h)


def forward_kernel(pieces, idx, *refs):
    parts = refs[:pieces]
    src, tgt, k, v, wq, wo, q, stats = refs[pieces : pieces + 8]
    outs = refs[pieces + 8 : 2 * pieces + 8]
    cat, bias, o = refs[2 * pieces + 8 :]
    inner = wq.shape[1]
    width = block_width(inner)
    join(idx, cat, parts)
    bias[...] = jnp.where(src[...] == tgt[...], 0.0, EXCLUDED).astype(F32)

    def project(at, g):
        q[:, at] = nn(cat[...], wq[:, at]).astype(BF16)

    blocks_of(inner, width, project)

    def head(at, h):
        weights, top, scale = softmax_terms(k[:, at], q[:, at], bias[...])
        stats[h, 0:1, :] = top
        stats[h, 1:2, :] = scale
        o[:, at] = tn((weights * scale).astype(BF16), v[:, at]).astype(BF16)

    head_loop(inner, head)

    for s in range(pieces):
        outs[s][...] = nn(o[...], wo[:, columns_of(idx, s, parts[0].shape[1])]).astype(outs[s].dtype)


def backward_kernel(pieces, idx, count, *refs):
    parts = refs[:pieces]
    src, tgt, q, k, v, stats, wq, wo, dk, dv = refs[pieces : pieces + 10]
    outs = refs[pieces + 10 : 2 * pieces + 10]
    cat, bias, do, dq = refs[2 * pieces + 10 :]
    inner = wq.shape[1]
    width = block_width(inner)
    valid = lax.broadcasted_iota(jnp.int32, parts[0].shape, 0) < count[0]
    join(idx, cat, parts, lambda x: jnp.where(valid, x, jnp.zeros_like(x)))
    bias[...] = jnp.where(src[...] == tgt[...], 0.0, EXCLUDED).astype(F32)

    def project(at, g):
        do[:, at] = nt(cat[...], wo[at, :]).astype(BF16)

    blocks_of(inner, width, project)

    def head(at, h):
        probs = jnp.exp(nt(k[:, at], q[:, at]) + bias[...] - stats[h, 0:1, :]) * stats[h, 1:2, :]
        grad_prob = nt(v[:, at], do[:, at])
        inner_sum = jnp.sum(probs * grad_prob, axis=0, keepdims=True)
        grad_score = (probs * (grad_prob - inner_sum)).astype(BF16)
        dq[:, at] = tn(grad_score, k[:, at]).astype(BF16)
        dk[:, at] = nn(grad_score, q[:, at]).astype(BF16)
        dv[:, at] = nn(probs.astype(BF16), do[:, at]).astype(BF16)

    head_loop(inner, head)

    for s in range(pieces):
        outs[s][...] = nt(dq[...], wq[columns_of(idx, s, parts[0].shape[1]), :]).astype(outs[s].dtype)


def memory_kernel(pieces, chunk, idx, dk, dv, wk, wv, keep, send, total):
    kept = keep.shape[1]
    mine, other = (pl.ds(pl.multiple_of(idx[pieces + i] * kept, kept), kept) for i in range(2))
    for s in range(pieces):
        rows = columns_of(idx, s, chunk)
        total[s] = nt(dk[...], wk[rows, :]) + nt(dv[...], wv[rows, :])
        keep[s] = total[s, mine, :]
        send[s] = total[s, other, :].astype(BF16)


def tree(values):
    while len(values) > 1:
        values = [values[i] + values[i + 1] for i in range(0, len(values), 2)]
    return values[0]


def add_up(own, arrived):
    total = own[...]
    for part in arrived:
        total = total + part[...].astype(F32)
    return total


def loss_kernel(count, own, *refs):
    arrived, (target, out, part) = refs[:-3], refs[-3:]
    low = add_up(own, arrived).astype(BF16)
    out[...] = low
    grad = jnp.where(lax.broadcasted_iota(jnp.int32, target.shape, 0) < count[0], target[...].astype(F32), 0.0)
    terms = jnp.sum(low.astype(F32) * grad, axis=0, keepdims=True)
    terms = jnp.broadcast_to(jnp.sum(terms, axis=1, keepdims=True), part.shape)
    first = lax.broadcasted_iota(jnp.int32, part.shape, 0) == 0
    part[...] = jnp.where(first, terms, count[0].astype(F32))


def high_low(x):
    high = x.astype(BF16).astype(F32)
    return high, (x - high).astype(BF16).astype(F32)


def join_kernel(pieces, keep, arrived, *refs):
    terms, outs, sums = refs[: -pieces - 1], refs[-pieces - 1 : -1], refs[-1]
    rows, columns = keep.shape[1], keep.shape[2]
    sums[...] = tree([term[...] for term in terms])
    extra = (EXTRA, columns)
    high, low = high_low(jnp.broadcast_to(sums[0:1, 0:1], extra))
    tail = jnp.where(lax.broadcasted_iota(jnp.int32, extra, 0) == 0, high, low).astype(BF16)
    outs[0][...] = keep[0] + arrived[0].astype(F32)
    for s in range(1, pieces):
        outs[s][0:rows, :] = (keep[s] + arrived[s].astype(F32)).astype(BF16)
        outs[s][rows : rows + EXTRA, :] = tail


def final_kernel(pieces, sums, *refs):
    own_m, arrived_m = refs[0], refs[1:pieces]
    own_x, arrived_x = refs[pieces], refs[pieces + 1 : 2 * pieces]
    grad_m, grad_x, loss = refs[2 * pieces :]
    rows = own_m.shape[0]
    count = sums[1:2, 0:1]
    grad_x[...] = (add_up(own_x, arrived_x) / count).astype(BF16)
    total = own_m[...]
    terms = [sum(high_low(sums[0:1, 0:1]))]
    for part in arrived_m:
        total = total + part[0:rows, :].astype(F32)
        tail = part[rows : rows + EXTRA, :].astype(F32)
        terms.append(tail[0:1, 0:1] + tail[1:2, 0:1])
    grad_m[...] = (total / count).astype(BF16)
    loss[...] = jnp.broadcast_to(tree(terms) / count, loss.shape)


EXTRA = 16
TILE = (8, 128)


def memory_whole_kernel(dk, dv, wk, wv, out):
    out[...] = nt(dk[...], wk[...]) + nt(dv[...], wv[...])


LOAD_PARTS = 8
HBM = pl.BlockSpec(memory_space=pltpu.HBM)
SMEM = pl.BlockSpec(memory_space=pltpu.SMEM)
VMEM = pl.BlockSpec(memory_space=pltpu.VMEM)


def head_group(inner):
    return min(8, inner // HEAD)


def params(mib):
    return pltpu.CompilerParams(vmem_limit_bytes=mib * 1024 * 1024)


def cost(flops, bytes_accessed, transcendentals=0):
    return pl.CostEstimate(flops=flops, bytes_accessed=bytes_accessed, transcendentals=transcendentals)


def piece_types(rows, chunk, which):
    return [jax.ShapeDtypeStruct((rows, chunk), F32 if s == 0 else BF16) for s in which]


def dims(parts, weight):
    rows, chunk = parts[0].shape
    features, inner = weight.shape
    return len(parts), rows, chunk, features, inner


def load(*weights):
    return pl.pallas_call(
        load_kernel,
        in_specs=[HBM] * len(weights),
        out_specs=[VMEM] * len(weights),
        out_shape=[pltpu.VMEM(w.shape, w.dtype) for w in weights],
        scratch_shapes=[pltpu.SemaphoreType.DMA((len(weights), LOAD_PARTS))],
        compiler_params=params(12),
        cost_estimate=cost(0, sum(2 * w.size for w in weights)),
        name="load",
    )(*weights)


def plain(kernel, out_types, *operands, smem=0, mib=12):
    return pl.pallas_call(
        kernel,
        in_specs=[SMEM] * smem + [VMEM] * (len(operands) - smem),
        out_specs=[VMEM] * len(out_types),
        out_shape=out_types,
        compiler_params=params(mib),
    )(*operands)


def project_kv(idx, parts, wk, wv):
    pieces, rows, _, features, inner = dims(parts, wk)
    return pl.pallas_call(
        functools.partial(kv_kernel, pieces),
        in_specs=[SMEM] + [VMEM] * (pieces + 2),
        out_specs=[VMEM, VMEM],
        out_shape=[jax.ShapeDtypeStruct((rows, inner), BF16)] * 2,
        scratch_shapes=[
            pltpu.VMEM((rows, features), BF16),
        ],
        compiler_params=params(12),
        cost_estimate=cost(4 * rows * features * inner, 4 * features * inner),
        name="project_kv",
    )(idx, *parts, wk, wv)


def attend(idx, parts, src, tgt, k, v, wq, wo):
    pieces, rows, chunk, features, inner = dims(parts, wq)
    src_len = k.shape[0]
    return pl.pallas_call(
        functools.partial(forward_kernel, pieces),
        in_specs=[SMEM] + [VMEM] * (pieces + 6),
        out_specs=[VMEM] * (2 + pieces),
        out_shape=[
            jax.ShapeDtypeStruct((rows, inner), BF16),
            jax.ShapeDtypeStruct((inner // HEAD, 2, rows), F32),
        ]
        + piece_types(rows, chunk, range(pieces)),
        scratch_shapes=[
            pltpu.VMEM((rows, features), BF16),
            pltpu.VMEM((src_len, rows), F32),
            pltpu.VMEM((rows, inner), BF16),
        ],
        compiler_params=params(12),
        cost_estimate=cost(6 * rows * features * inner, 8 * features * inner),
        name="attend",
    )(idx, *parts, src, tgt, k, v, wq, wo)


def attend_backward(idx, count, parts, src, tgt, q, k, v, stats, wq, wo):
    pieces, rows, chunk, features, inner = dims(parts, wq)
    src_len = k.shape[0]
    return pl.pallas_call(
        functools.partial(backward_kernel, pieces),
        in_specs=[SMEM, SMEM] + [VMEM] * (pieces + 8),
        out_specs=[VMEM] * (2 + pieces),
        out_shape=[jax.ShapeDtypeStruct((src_len, inner), BF16)] * 2 + piece_types(rows, chunk, range(pieces)),
        scratch_shapes=[
            pltpu.VMEM((rows, features), BF16),
            pltpu.VMEM((src_len, rows), F32),
            pltpu.VMEM((rows, inner), BF16),
            pltpu.VMEM((rows, inner), BF16),
        ],
        compiler_params=params(12),
        cost_estimate=cost(8 * rows * features * inner, 8 * features * inner),
        name="attend_backward",
    )(idx, count, *parts, src, tgt, q, k, v, stats, wq, wo)


def memory_grads(idx, pieces, chunk, dk, dv, wk, wv):
    rows, inner = dk.shape
    return pl.pallas_call(
        functools.partial(memory_kernel, pieces, chunk),
        in_specs=[SMEM] + [VMEM] * 4,
        out_specs=[VMEM] * 2,
        out_shape=[
            jax.ShapeDtypeStruct((pieces, rows // 2, chunk), F32),
            jax.ShapeDtypeStruct((pieces, rows // 2, chunk), BF16),
        ],
        scratch_shapes=[
            pltpu.VMEM((pieces, rows, chunk), F32),
        ],
        compiler_params=params(12),
        cost_estimate=cost(4 * rows * chunk * pieces * inner, 4 * chunk * pieces * inner),
        name="memory_grads",
    )(idx, dk, dv, wk, wv)


def memory_grads_whole(dk, dv, wk, wv):
    return pl.pallas_call(
        memory_whole_kernel,
        in_specs=[VMEM] * 4,
        out_specs=VMEM,
        out_shape=jax.ShapeDtypeStruct((dk.shape[0], wk.shape[0]), F32),
        compiler_params=params(16),
        name="memory_grads_whole",
    )(dk, dv, wk, wv)


def swap(x, axis, step):
    size = lax.axis_size(axis)
    return lax.ppermute(x, axis, [(i, i ^ step) for i in range(size)])


def after(first, then):
    return lax.optimization_barrier((first, then))


def local(direct, memory, states, targets, w_query, w_key, w_value, w_out, src_ids, tgt_ids, counts):
    run = local_direct if direct else local_gathered
    src, tgt = src_ids.reshape(-1, 1), tgt_ids.reshape(1, -1)
    out, loss, grad_x, grad_m = run(
        memory[0],
        states[0, 0],
        targets[0, 0],
        w_query[0],
        w_key[0],
        w_value[0],
        w_out[0],
        src,
        tgt,
        counts,
    )
    return out[None, None], loss.reshape(1), grad_x[None, None], grad_m[None]


def local_gathered(mem, state, target, wq, wk, wv, wo, src, tgt, counts):
    idx = jnp.zeros((1,), jnp.int32)

    def gather(x):
        return [lax.all_gather(x, "mp", axis=1, tiled=True)]

    def scatter(x):
        return lax.psum_scatter(x, "mp", scatter_dimension=1, tiled=True)

    k, v = project_kv(idx, gather(mem), wk, wv)
    q, stats, out_part = attend(idx, gather(state), src, tgt, k, v, wq, wo)
    out_low = scatter(out_part).astype(BF16)
    dk, dv, grad_x_part = attend_backward(idx, counts, gather(target), src, tgt, q, k, v, stats, wq, wo)
    grad_m = lax.psum(scatter(memory_grads_whole(dk, dv, wk, wv)), "phase")
    valid = jnp.arange(target.shape[0])[:, None] < counts[0]
    loss_part = jnp.sum(jnp.where(valid, out_low.astype(F32) * target.astype(F32), 0.0))
    count_part = counts[0].astype(F32) / lax.axis_size("mp")
    loss_total, count_total = lax.psum((loss_part, count_part), ("dp", "mp"))
    grad_x = (scatter(grad_x_part) / count_total).astype(BF16)
    return out_low, loss_total / count_total, grad_x, (grad_m / count_total).astype(BF16)


def local_direct(mem, state, target, wq, wk, wv, wo, src, tgt, counts):
    n = lax.axis_size("mp")
    steps = range(n - 1, 0, -1)
    phase = lax.axis_index("phase")
    order = jnp.arange(n + 2, dtype=jnp.int32)
    idx = jnp.where(order < n, lax.axis_index("mp") ^ order, phase ^ (order - n))
    chunk = mem.shape[1]

    def exchange(parts):
        moved = {}
        for s in steps:
            moved[s] = swap(parts[s], "mp", s)
        return [moved[s] for s in range(1, n)]

    mem_parts = [mem] + exchange([mem] * n)
    weights = [pltpu.with_memory_space_constraint(w, pltpu.HBM) for w in (wk, wv)]
    idx, weights = after(idx, weights)
    wk, wv = load(*weights)
    mem_parts, state = after(mem_parts, state)
    state_parts = [state] + exchange([state] * n)
    k, v = project_kv(idx, mem_parts, wk, wv)
    weights = [pltpu.with_memory_space_constraint(w, pltpu.HBM) for w in (wq, wo)]
    k, weights = after(k, weights)
    wq, wo = load(*weights)
    state_parts, target = after(state_parts, target)
    target_parts = [target] + exchange([target] * n)
    q, stats, *out_parts = attend(idx, state_parts, src, tgt, k, v, wq, wo)
    out_arrived = exchange(out_parts)
    dk, dv, *grad_x_parts = attend_backward(
        idx, counts, target_parts, src, tgt, q, k, v, stats, wq, wo
    )
    grad_x_arrived = exchange(grad_x_parts)
    keep, send = memory_grads(idx, n, chunk, dk, dv, wk, wv)
    out_arrived, keep = after(out_arrived, keep)
    rows, kept = mem.shape[0], keep.shape[1]
    send_arrived = swap(send, "phase", 1)
    out_low, part = plain(
        loss_kernel,
        [jax.ShapeDtypeStruct((rows, chunk), BF16), jax.ShapeDtypeStruct(TILE, F32)],
        counts,
        out_parts[0],
        *out_arrived,
        target,
        smem=1,
    )
    terms = [part] + [swap(part, "dp", s) for s in range(1, lax.axis_size("dp"))]
    *grad_m_parts, sums = plain(
        functools.partial(join_kernel, n),
        [jax.ShapeDtypeStruct((kept, chunk), F32)]
        + [jax.ShapeDtypeStruct((kept + EXTRA, chunk), BF16)] * (n - 1)
        + [jax.ShapeDtypeStruct(TILE, F32)],
        keep,
        send_arrived,
        *terms,
    )
    grad_m_arrived = exchange(grad_m_parts)
    grad_m_half, grad_x, loss = plain(
        functools.partial(final_kernel, n),
        [
            jax.ShapeDtypeStruct((kept, chunk), BF16),
            jax.ShapeDtypeStruct((rows, chunk), BF16),
            jax.ShapeDtypeStruct(TILE, F32),
        ],
        sums,
        grad_m_parts[0],
        *grad_m_arrived,
        grad_x_parts[0],
        *grad_x_arrived,
    )
    grad_m_other = swap(grad_m_half, "phase", 1)
    first = phase == 0
    grad_m = jnp.concatenate(
        [jnp.where(first, grad_m_half, grad_m_other), jnp.where(first, grad_m_other, grad_m_half)], axis=0
    )
    return out_low, loss[0, 0], grad_x, grad_m


def power_of_two(size):
    return size & (size - 1) == 0


def solution(mesh):
    sizes = mesh.shape
    placed = (
        P("dp", None, "mp"),
        P("phase", "dp", None, "mp"),
        P("phase", "dp", None, "mp"),
        P("phase", None, "mp"),
        P("phase", None, "mp"),
        P("phase", None, "mp"),
        P("phase", "mp", None),
        P("dp", None),
        P("dp", None),
        P("dp"),
    )
    direct = 1 < sizes["mp"] <= 4 and power_of_two(sizes["mp"]) and power_of_two(sizes["dp"]) and sizes["phase"] == 2
    return jax.shard_map(
        functools.partial(local, direct),
        mesh=mesh,
        in_specs=placed,
        out_specs=(
            P("phase", "dp", None, "mp"),
            P("phase"),
            P("phase", "dp", None, "mp"),
            P("dp", None, "mp"),
        ),
        check_vma=False,
    )
```
